32 devices in a mesh: mem: 16 (over z, y, x), patch: 2 (over core).
Axes of the slice: x: 2, y: 2, z: 4, core: 2. Of those that a mesh axis runs over, the one named last changes fastest.
Arguments:
- state: bfloat16 [3, 1024, 8192], P(None, 'mem', 'patch'), may hold values from -6 to 6
- obs_noise: bfloat16 [1024, 8192], P('mem', 'patch'), may hold values from -6 to 6
- obs_values: float32 [2, 4096], P('patch', 'mem'), may hold values from -6 to 6
- obs_weights: bfloat16 [2, 32, 128, 128], P('patch', 'mem'), may hold values from -1 to 1
- tapers: float32 [8, 128, 128], replicated, may hold values from 0.2 to 1
- pair_source: int32 [2, 32, 4], P('patch', 'mem'), may hold values from 0 to 31, as said below
- pair_taper: int32 [2, 32, 4], P('patch', 'mem'), may hold values from 0 to 7
Outputs:
- analysis: bfloat16 [3, 1024, 8192], P(None, 'mem', 'patch')
The draws below stay inside these ranges and needn't reach their ends.
Inputs may be any that keep to these rules, and one draw needn't show every extreme that they name: `pair_source`: each listed source lies in the same patch within 2 blocks of its target block; positions beyond the patch's ends are moved to its first or last block.
All inputs are finite; a program needn't handle non-finite values.
Results may differ from the reference program's by a relative error of at most 0.0058.
Values may be sent and summed in bfloat16 or wider, within the bound.
A program may use at most 64 MiB of HBM per device.

```python
import jax
import jax.numpy as jnp
from jax import lax

MEMBERS = 1024
VARIABLES = 3
BLOCK_CELLS = 128
RADIUS = 2
PAIRS = 4
TAPERS = 8
PATCHES = 2
PATCH_BLOCKS = 32
PATCH_CELLS = 4096
TOTAL_CELLS = 8192


def draw_obs_weights(key, part):
    first_key, second_key = jax.random.split(jax.random.fold_in(key, 17))
    shape = (PATCHES, PATCH_BLOCKS, BLOCK_CELLS, BLOCK_CELLS)
    diagonal = jnp.exp(jax.random.uniform(first_key, shape[:3], jnp.float32, jnp.log(0.3), 0.0))
    spread = jax.random.normal(second_key, shape, jnp.float32)
    offdiag = jnp.clip(spread * 0.5 / jnp.sqrt(1.0 * BLOCK_CELLS), -0.3, 0.3)
    unit = jnp.eye(BLOCK_CELLS, dtype=jnp.float32)
    weights = offdiag * (1.0 - unit) + unit * diagonal[..., None]
    return weights.astype(jnp.bfloat16)


def draw_pair_source(key, part):
    width = 2 * RADIUS + 1
    scores = jax.random.randint(jax.random.fold_in(key, 29), (PATCHES, PATCH_BLOCKS, width), 0, 4096)
    scores = scores * 8 + jnp.arange(width, dtype=jnp.int32)
    order = jnp.argsort(scores, axis=-1, stable=True)[..., :PAIRS].astype(jnp.int32)
    target = jnp.arange(PATCH_BLOCKS, dtype=jnp.int32)[None, :, None]
    source = jnp.clip(target + order - RADIUS, 0, PATCH_BLOCKS - 1)
    return source.astype(jnp.int32)


def plant(drawn, own_key, smallest, high):
    extent = drawn.shape
    index_at = [jax.random.randint(jax.random.fold_in(own_key, axis), (), 0, extent[axis]) for axis in range(len(extent))]
    drawn = drawn.at[tuple(index_at)].set(smallest)
    longest = extent.index(max(extent))
    index_at[longest] = (index_at[longest] + 1) % extent[longest]
    return drawn.at[tuple(index_at)].set(high)


def shard_levels(own_key, shape, shards, least, top_value):
    loudness, own = 1.0, jax.random.fold_in(own_key, 6)
    for axis_at, parts in shards:
        heights = jnp.exp(jax.random.uniform(jax.random.fold_in(own, axis_at), (parts,), jnp.float32, least / len(shards), top_value / len(shards)))
        loudness = loudness * jnp.repeat(heights, shape[axis_at] // parts).reshape([-1 if axis == axis_at else 1 for axis in range(len(shape))])
    return loudness


def normal_values(own_key, dims, deviation, reach, cuts=(), held_as=jnp.bfloat16):
    entries = jax.random.normal(own_key, dims, jnp.float32) * deviation
    if len(cuts) > 0:
        entries = shard_levels(own_key, dims, cuts, -0.22, 0.18) * entries
    return jnp.clip(entries, min=-reach, max=reach).astype(held_as)


def setup_inputs(seed: int = 0) -> dict:
    arg_keys = jax.random.split(jax.random.key(seed), 8)
    state = normal_values(arg_keys[0], (VARIABLES, MEMBERS, TOTAL_CELLS), 1.0, 6.0, ((1, 16), (2, 2)))
    obs_noise = normal_values(arg_keys[1], (MEMBERS, TOTAL_CELLS), 1.0, 6.0, ((0, 16), (1, 2)))
    obs_values = normal_values(arg_keys[2], (PATCHES, PATCH_CELLS), 1.0, 6.0, ((0, 2), (1, 16)), jnp.float32)
    obs_weights = draw_obs_weights(jax.random.fold_in(arg_keys[7], 71), 0)
    tapers = jnp.clip(jax.random.uniform(arg_keys[4], (TAPERS, BLOCK_CELLS, BLOCK_CELLS), jnp.float32, 0.2, 1.0), 0.2, 1.0)
    pair_source = draw_pair_source(jax.random.fold_in(arg_keys[7], 71), 0)
    pair_taper = plant(jax.random.randint(arg_keys[6], (PATCHES, PATCH_BLOCKS, PAIRS), 0, TAPERS), jax.random.fold_in(arg_keys[6], 1), 0, TAPERS - 1).astype(jnp.int32)
    return {"state": state, "obs_noise": obs_noise, "obs_values": obs_values, "obs_weights": obs_weights, "tapers": tapers, "pair_source": pair_source, "pair_taper": pair_taper}


def reference(state, obs_noise, obs_values, obs_weights, tapers, pair_source, pair_taper):
    grid = state.reshape(VARIABLES, MEMBERS, PATCHES, PATCH_BLOCKS, BLOCK_CELLS).astype(jnp.float32)
    center = jnp.mean(grid, axis=1, keepdims=True)
    anomaly = (grid - center).astype(jnp.bfloat16)
    noise_grid = obs_noise.reshape(MEMBERS, PATCHES, PATCH_BLOCKS, BLOCK_CELLS).astype(jnp.float32)
    observed = obs_values.reshape(PATCHES, PATCH_BLOCKS, BLOCK_CELLS)
    innovation = (observed[None] + noise_grid - grid[0]).astype(jnp.bfloat16)
    weighted = jnp.einsum("pbcd,npbd->npbc", obs_weights.astype(jnp.float32),
                          innovation.astype(jnp.float32)).astype(jnp.bfloat16)

    def per_patch(patch):
        anom_patch = anomaly[:, :, patch]
        weight_patch = weighted[:, patch]
        source_patch = pair_source[patch]
        taper_patch = pair_taper[patch]

        def per_target(target):
            target_anom = anom_patch[:, :, target].astype(jnp.float32)
            total = jnp.zeros((VARIABLES, MEMBERS, BLOCK_CELLS), jnp.float32)
            for slot in range(PAIRS):
                source = source_patch[target, slot]
                source_anom = anom_patch[0, :, source].astype(jnp.float32)
                source_weight = weight_patch[:, source].astype(jnp.float32)
                taper = tapers[taper_patch[target, slot]]
                covariance = jnp.einsum("vnc,nd->vcd", target_anom, source_anom) / (MEMBERS - 1)
                localized = (taper * covariance).astype(jnp.bfloat16)
                total = total + jnp.einsum("nd,vcd->vnc", source_weight, localized.astype(jnp.float32))
            return total

        return lax.map(per_target, jnp.arange(PATCH_BLOCKS, dtype=jnp.int32))

    increment = lax.map(per_patch, jnp.arange(PATCHES, dtype=jnp.int32))
    increment = jnp.transpose(increment, (2, 3, 0, 1, 4)).reshape(VARIABLES, MEMBERS, TOTAL_CELLS)
    return (state.astype(jnp.float32) + increment).astype(jnp.bfloat16)
```

```python
import functools

import jax
import jax.numpy as jnp
from jax import lax
from jax.experimental import pallas as pl
from jax.experimental.pallas import tpu as pltpu
from jax.sharding import PartitionSpec as P

RADIUS = 2
MESH = pl.DeviceIdType.MESH


def kernel(
    n,
    state, noise, obs_values, obs_weights, tapers, pair_source, pair_taper,
    out,
    rin, win_at, win_w, anom, local_t, taper_t, outbuf,
    in_send, in_recv, local_sem, halo_send, halo_recv, out_send, out_recv,
):
    me = lax.axis_index("mem")
    part = lax.axis_index("patch")
    variables, rows, _ = state.shape
    members, owned = rin.shape[1], rin.shape[2]
    blocks = obs_weights.shape[1]
    size = obs_weights.shape[2]
    pairs = pair_source.shape[2]
    kinds = rin.shape[0]
    wide = variables * size

    barrier = pltpu.get_barrier_semaphore()

    def greet(k, _):
        peer = lax.rem(me + k, n)
        pl.semaphore_signal(barrier, inc=1, device_id=(peer, part), device_id_type=MESH)
        return 0

    lax.fori_loop(1, n, greet, 0)

    def source(kind, owner):
        columns = pl.ds(pl.multiple_of(owner * owned, owned), owned)
        return noise.at[:, columns] if kind == 1 else state.at[max(kind - 1, 0), :, columns]

    my_rows = pl.ds(pl.multiple_of(me * rows, rows), rows)
    locals_ = [
        pltpu.make_async_copy(source(kind, me), rin.at[kind, my_rows], local_sem.at[kind])
        for kind in range(kinds)
    ]
    for copy in locals_:
        copy.start()
    pl.semaphore_wait(barrier, n - 1)

    for kind in range(kinds):
        def send(k, _, kind=kind):
            peer = lax.rem(me + k, n)
            pltpu.make_async_remote_copy(
                src_ref=source(kind, peer),
                dst_ref=rin.at[kind, my_rows],
                send_sem=in_send.at[kind],
                recv_sem=in_recv.at[kind],
                device_id=(peer, part),
                device_id_type=MESH,
            ).start()
            return 0

        lax.fori_loop(1, n, send, 0)

    for k in range(tapers.shape[0]):
        taper_t[k] = tapers[k].T * (1.0 / (members - 1))

    remote_rows = (n - 1) * rows

    def arrived(kind):
        locals_[kind].wait()
        block = rin.at[kind, pl.ds(0, remote_rows)]
        pltpu.make_async_copy(block, block, in_recv.at[kind]).wait()

    def centered(kind):
        values = rin[kind].astype(jnp.float32)
        center = jnp.sum(values, axis=0, keepdims=True) * (1.0 / members)
        return (values - center).astype(jnp.bfloat16)

    arrived(0)
    first = centered(0)
    for b in range(blocks):
        tile = first[:, b * size : (b + 1) * size]
        anom[b, :, 0:size] = tile
        win_at[RADIUS + b] = tile.T

    own = pl.ds(RADIUS, blocks)
    halo = []

    def exchange(window, index):
        left = pltpu.make_async_remote_copy(
            src_ref=window.at[own],
            dst_ref=window.at[pl.ds(RADIUS + blocks, blocks)],
            send_sem=halo_send.at[index, 0],
            recv_sem=halo_recv.at[index, 0],
            device_id=(jnp.maximum(me - 1, 0), part),
            device_id_type=MESH,
        )
        right = pltpu.make_async_remote_copy(
            src_ref=window.at[own],
            dst_ref=window.at[pl.ds(0, blocks)],
            send_sem=halo_send.at[index, 1],
            recv_sem=halo_recv.at[index, 1],
            device_id=(jnp.minimum(me + 1, n - 1), part),
            device_id_type=MESH,
        )

        @pl.when(me > 0)
        def _():
            left.start()

        @pl.when(me < n - 1)
        def _():
            right.start()

        halo.append((left, right))

    exchange(win_at, 0)
    arrived(1)
    innovation = (
        obs_values[...] + rin[1].astype(jnp.float32) - rin[0].astype(jnp.float32)
    ).astype(jnp.bfloat16)
    for b in range(blocks):
        win_w[RADIUS + b] = lax.dot_general(
            innovation[:, b * size : (b + 1) * size],
            obs_weights[0, b],
            (((1,), (1,)), ((), ())),
            preferred_element_type=jnp.float32,
        ).astype(jnp.bfloat16)
    exchange(win_w, 1)

    for kind in range(2, kinds):
        arrived(kind)
        values = centered(kind)
        for b in range(blocks):
            anom[b, :, (kind - 1) * size : kind * size] = values[:, b * size : (b + 1) * size]

    def landed(index):
        left, right = halo[index]

        @pl.when(me > 0)
        def _():
            left.wait_send()
            right.wait_recv()

        @pl.when(me < n - 1)
        def _():
            right.wait_send()
            left.wait_recv()

    landed(0)
    base = me * blocks - RADIUS

    def slot(b, j):
        return jnp.clip(pair_source[0, b, j] - base, 0, win_at.shape[0] - 1)

    for b in range(blocks):
        def pair(j, _, b=b):
            at = win_at[slot(b, j)]
            covariance = jnp.dot(at, anom[b], preferred_element_type=jnp.float32)
            taper = taper_t[pair_taper[0, b, j]]
            local_t[b, pl.ds(pl.multiple_of(j * size, size), size), :] = (
                covariance * jnp.concatenate([taper] * variables, axis=1)
            ).astype(jnp.bfloat16)
            return 0

        lax.fori_loop(0, pairs, pair, 0)

    landed(1)
    chunk = 256
    chunks = members // chunk
    per = chunk // rows
    mine = pl.ds(pl.multiple_of(me * owned, owned), owned)

    def answer(i, _):
        at = lax.rem(i + me // per, chunks)
        here = pl.ds(pl.multiple_of(at * chunk, chunk), chunk)
        for b in range(blocks):
            weights = jnp.concatenate(
                [win_w[slot(b, j), here, :] for j in range(pairs)], axis=1
            )
            increment = jnp.dot(weights, local_t[b], preferred_element_type=jnp.float32)
            for v in range(variables):
                kind = v + 1 if v else 0
                part_of = slice(b * size, (b + 1) * size)
                outbuf[v, here, part_of] = (
                    rin[kind, here, part_of].astype(jnp.float32)
                    + increment[:, v * size : (v + 1) * size]
                ).astype(jnp.bfloat16)

        def give(k, _):
            peer = at * per + lax.rem(k + me, per)
            theirs = pl.ds(pl.multiple_of(peer * rows, rows), rows)

            @pl.when(peer != me)
            def _():
                pltpu.make_async_remote_copy(
                    src_ref=outbuf.at[:, theirs, :],
                    dst_ref=out.at[:, :, mine],
                    send_sem=out_send,
                    recv_sem=out_recv,
                    device_id=(peer, part),
                    device_id_type=MESH,
                ).start()

            return 0

        lax.fori_loop(0, per, give, 0)
        return 0

    lax.fori_loop(0, chunks, answer, 0)
    keep = pltpu.make_async_copy(outbuf.at[:, my_rows, :], out.at[:, :, mine], local_sem.at[kinds])
    keep.start()
    keep.wait()
    for kind in range(kinds):
        block = rin.at[kind, pl.ds(0, remote_rows)]
        pltpu.make_async_copy(block, block, in_send.at[kind]).wait()
    block = outbuf.at[:, pl.ds(0, remote_rows), :]
    pltpu.make_async_copy(block, block, out_send).wait()
    pltpu.make_async_copy(block, block, out_recv).wait()


def on_device(n, state, obs_noise, obs_values, obs_weights, tapers, pair_source, pair_taper):
    variables, rows, cells = state.shape
    members = rows * n
    owned = cells // n
    blocks, size = obs_weights.shape[1], obs_weights.shape[2]
    pairs = pair_source.shape[2]
    window = blocks + 2 * RADIUS
    anywhere = pl.BlockSpec(memory_space=pl.ANY)
    vmem = pl.BlockSpec(memory_space=pltpu.VMEM)
    smem = pl.BlockSpec(memory_space=pltpu.SMEM)
    kinds = variables + 1
    return pl.pallas_call(
        functools.partial(kernel, n),
        out_shape=jax.ShapeDtypeStruct(state.shape, state.dtype),
        in_specs=[anywhere, anywhere, vmem, vmem, vmem, smem, smem],
        out_specs=anywhere,
        scratch_shapes=[
            pltpu.VMEM((kinds, members, owned), jnp.bfloat16),
            pltpu.VMEM((window, size, members), jnp.bfloat16),
            pltpu.VMEM((window, members, size), jnp.bfloat16),
            pltpu.VMEM((blocks, members, variables * size), jnp.bfloat16),
            pltpu.VMEM((blocks, pairs * size, variables * size), jnp.bfloat16),
            pltpu.VMEM(tapers.shape, jnp.float32),
            pltpu.VMEM((variables, members, owned), jnp.bfloat16),
            pltpu.SemaphoreType.DMA((kinds,)),
            pltpu.SemaphoreType.DMA((kinds,)),
            pltpu.SemaphoreType.DMA((kinds + 1,)),
            pltpu.SemaphoreType.DMA((2, 2)),
            pltpu.SemaphoreType.DMA((2, 2)),
            pltpu.SemaphoreType.DMA,
            pltpu.SemaphoreType.DMA,
        ],
        compiler_params=pltpu.CompilerParams(collective_id=0, has_side_effects=True),
    )(state, obs_noise, obs_values, obs_weights, tapers, pair_source, pair_taper)


def solution(mesh):
    placed = (
        P(None, "mem", "patch"),
        P("mem", "patch"),
        P("patch", "mem"),
        P("patch", "mem", None, None),
        P(),
        P("patch", "mem", None),
        P("patch", "mem", None),
    )
    return jax.shard_map(
        functools.partial(on_device, mesh.shape["mem"]),
        mesh=mesh,
        in_specs=placed,
        out_specs=P(None, "mem", "patch"),
        check_vma=False,
    )
```

```python
import functools

import jax
import jax.numpy as jnp
from jax import lax
from jax.experimental import pallas as pl
from jax.experimental.pallas import tpu as pltpu
from jax.sharding import PartitionSpec as P

RADIUS = 2
MESH = pl.DeviceIdType.MESH


def gray(q):
    return q + (q // 2) * (1 - 2 * (q % 2))


def device_of(rank, part):
    level, q = rank // 4, rank % 4
    q = q + (level % 2) * (3 - 2 * q)
    spot = gray(q)
    return level * 4 + spot + (part % 2) * (3 - 2 * spot)


def rank_of(device, part):
    level, spot = device // 4, device % 4
    spot = spot + (part % 2) * (3 - 2 * spot)
    q = gray(spot)
    return level * 4 + q + (level % 2) * (3 - 2 * q)


def kernel(
    n,
    state, noise, obs_values, obs_weights, tapers, pair_source, pair_taper,
    out,
    rin, win_at, win_w, anom, local_t, taper_in, taper_t, outbuf, weights_in, values_in, source_in, choice_in,
    in_send, in_recv, local_sem, halo_send, halo_recv, out_send, out_recv, small_send, small_recv,
):
    me = lax.axis_index("mem")
    part = lax.axis_index("patch")
    variables, rows, _ = state.shape
    members, owned = rin.shape[1], rin.shape[2]
    blocks, size, _ = weights_in.shape
    pairs = source_in.shape[1]
    kinds = rin.shape[0]
    rank = rank_of(me, part)

    barrier = pltpu.get_barrier_semaphore()

    def greet(k, _):
        peer = lax.rem(me + k, n)
        pl.semaphore_signal(barrier, inc=1, device_id=(peer, part), device_id_type=MESH)
        return 0

    lax.fori_loop(1, n, greet, 0)

    def source(kind, owner):
        columns = pl.ds(pl.multiple_of(owner * owned, owned), owned)
        return noise.at[:, columns] if kind == 1 else state.at[max(kind - 1, 0), :, columns]

    my_rows = pl.ds(pl.multiple_of(me * rows, rows), rows)
    locals_ = [
        pltpu.make_async_copy(source(kind, rank), rin.at[kind, my_rows], local_sem.at[kind])
        for kind in range(kinds)
    ]
    for copy in locals_:
        copy.start()
    taper_copy = pltpu.make_async_copy(tapers, taper_in, local_sem.at[kinds])
    taper_copy.start()
    pl.semaphore_wait(barrier, n - 1)

    def send_kind(kind):
        def send(k, _):
            peer = lax.rem(me + k, n)
            pltpu.make_async_remote_copy(
                src_ref=source(kind, rank_of(peer, part)),
                dst_ref=rin.at[kind, my_rows],
                send_sem=in_send.at[kind],
                recv_sem=in_recv.at[kind],
                device_id=(peer, part),
                device_id_type=MESH,
            ).start()
            return 0

        lax.fori_loop(1, n, send, 0)

    send_kind(0)
    keeper = device_of(me, part)
    small = [
        (obs_weights.at[0], weights_in),
        (obs_values, values_in),
        (pair_source.at[0], source_in),
        (pair_taper.at[0], choice_in),
    ]

    def small_remote(i):
        return pltpu.make_async_remote_copy(
            src_ref=small[i][0],
            dst_ref=small[i][1],
            send_sem=small_send.at[i],
            recv_sem=small_recv.at[i],
            device_id=(keeper, part),
            device_id_type=MESH,
        )

    def small_local(i):
        return pltpu.make_async_copy(small[i][0], small[i][1], small_recv.at[i])

    @pl.when(keeper != me)
    def _():
        for i in range(len(small)):
            small_remote(i).start()

    @pl.when(keeper == me)
    def _():
        for i in range(len(small)):
            small_local(i).start()

    send_kind(1)

    taper_copy.wait()
    for k in range(tapers.shape[0]):
        taper_t[k] = taper_in[k].T * (1.0 / (members - 1))

    remote_rows = (n - 1) * rows

    def arrived(kind):
        locals_[kind].wait()
        block = rin.at[kind, pl.ds(0, remote_rows)]
        pltpu.make_async_copy(block, block, in_recv.at[kind]).wait()

    def centered(kind):
        values = rin[kind].astype(jnp.float32)
        center = jnp.sum(values, axis=0, keepdims=True) * (1.0 / members)
        return (values - center).astype(jnp.bfloat16)

    own = pl.ds(RADIUS, blocks)
    halo = []

    def exchange(window, index):
        left = pltpu.make_async_remote_copy(
            src_ref=window.at[own],
            dst_ref=window.at[pl.ds(RADIUS + blocks, blocks)],
            send_sem=halo_send.at[index, 0],
            recv_sem=halo_recv.at[index, 0],
            device_id=(device_of(jnp.maximum(rank - 1, 0), part), part),
            device_id_type=MESH,
        )
        right = pltpu.make_async_remote_copy(
            src_ref=window.at[own],
            dst_ref=window.at[pl.ds(0, blocks)],
            send_sem=halo_send.at[index, 1],
            recv_sem=halo_recv.at[index, 1],
            device_id=(device_of(jnp.minimum(rank + 1, n - 1), part), part),
            device_id_type=MESH,
        )

        @pl.when(rank > 0)
        def _():
            left.start()

        @pl.when(rank < n - 1)
        def _():
            right.start()

        halo.append((left, right))

    def landed(index):
        left, right = halo[index]

        @pl.when(rank > 0)
        def _():
            left.wait_send()
            right.wait_recv()

        @pl.when(rank < n - 1)
        def _():
            right.wait_send()
            left.wait_recv()

    arrived(0)
    first = centered(0)
    anom[0] = first
    for b in range(blocks):
        win_at[RADIUS + b] = first[:, b * size : (b + 1) * size].T
    exchange(win_at, 0)
    send_kind(2)

    @pl.when(keeper != me)
    def _():
        for i in range(len(small)):
            small_remote(i).wait()

    @pl.when(keeper == me)
    def _():
        for i in range(len(small)):
            small_local(i).wait()

    arrived(1)
    innovation = (
        values_in[...] + rin[1].astype(jnp.float32) - rin[0].astype(jnp.float32)
    ).astype(jnp.bfloat16)
    for b in range(blocks):
        win_w[RADIUS + b] = lax.dot_general(
            innovation[:, b * size : (b + 1) * size],
            weights_in[b],
            (((1,), (1,)), ((), ())),
            preferred_element_type=jnp.float32,
        ).astype(jnp.bfloat16)
    exchange(win_w, 1)
    for kind in range(3, kinds):
        send_kind(kind)

    base = rank * blocks - RADIUS

    def slot(b, j):
        return jnp.clip(source_in[b, j] - base, 0, win_at.shape[0] - 1)

    chunks = 4
    chunk = members // chunks
    per = chunk // rows
    mine = pl.ds(pl.multiple_of(rank * owned, owned), owned)
    quarter = me // per
    half, odd = quarter // 2, quarter % 2

    def localize(v):
        for b in range(blocks):
            def pair(j, _, b=b):
                covariance = jnp.dot(
                    win_at[slot(b, j)],
                    anom[v, :, b * size : (b + 1) * size],
                    preferred_element_type=jnp.float32,
                )
                local_t[v, b, pl.ds(pl.multiple_of(j * size, size), size), :] = (
                    covariance * taper_t[choice_in[b, j]]
                ).astype(jnp.bfloat16)
                return 0

            lax.fori_loop(0, pairs, pair, 0)

    def answer(v):
        kind = v + 1 if v else 0

        def step(i, _):
            over, flip = i // 2, (i + i // 2) % 2
            at = 2 * (1 - over + (2 * over - 1) * half) + flip + (1 - 2 * flip) * odd
            here = pl.ds(pl.multiple_of(at * chunk, chunk), chunk)
            for b in range(blocks):
                weights = jnp.concatenate(
                    [win_w[slot(b, j), here, :] for j in range(pairs)], axis=1
                )
                increment = jnp.dot(weights, local_t[v, b], preferred_element_type=jnp.float32)
                part_of = slice(b * size, (b + 1) * size)
                outbuf[v, here, part_of] = (
                    rin[kind, here, part_of].astype(jnp.float32) + increment
                ).astype(jnp.bfloat16)

            def give(k, _):
                peer = at * per + lax.rem(k + me, per)
                theirs = pl.ds(pl.multiple_of(peer * rows, rows), rows)

                @pl.when(peer != me)
                def _():
                    pltpu.make_async_remote_copy(
                        src_ref=outbuf.at[v, theirs, :],
                        dst_ref=out.at[v, :, mine],
                        send_sem=out_send,
                        recv_sem=out_recv,
                        device_id=(peer, part),
                        device_id_type=MESH,
                    ).start()

                return 0

            lax.fori_loop(0, per, give, 0)
            return 0

        lax.fori_loop(0, chunks, step, 0)

    for v in range(variables):
        if v:
            arrived(v + 1)
            anom[v] = centered(v + 1)
        else:
            landed(0)
        localize(v)
        if not v:
            landed(1)
        answer(v)

    keep = pltpu.make_async_copy(outbuf.at[:, my_rows, :], out.at[:, :, mine], local_sem.at[kinds + 1])
    keep.start()
    keep.wait()
    for kind in range(kinds):
        block = rin.at[kind, pl.ds(0, remote_rows)]
        pltpu.make_async_copy(block, block, in_send.at[kind]).wait()
    block = outbuf.at[:, pl.ds(0, remote_rows), :]
    pltpu.make_async_copy(block, block, out_send).wait()
    pltpu.make_async_copy(block, block, out_recv).wait()


def on_device(n, state, obs_noise, obs_values, obs_weights, tapers, pair_source, pair_taper):
    variables, rows, cells = state.shape
    members = rows * n
    owned = cells // n
    blocks, size = obs_weights.shape[1], obs_weights.shape[2]
    pairs = pair_source.shape[2]
    window = blocks + 2 * RADIUS
    anywhere = pl.BlockSpec(memory_space=pl.ANY)
    kinds = variables + 1
    return pl.pallas_call(
        functools.partial(kernel, n),
        out_shape=jax.ShapeDtypeStruct(state.shape, state.dtype),
        in_specs=[anywhere] * 7,
        out_specs=anywhere,
        scratch_shapes=[
            pltpu.VMEM((kinds, members, owned), jnp.bfloat16),
            pltpu.VMEM((window, size, members), jnp.bfloat16),
            pltpu.VMEM((window, members, size), jnp.bfloat16),
            pltpu.VMEM((variables, members, owned), jnp.bfloat16),
            pltpu.VMEM((variables, blocks, pairs * size, size), jnp.bfloat16),
            pltpu.VMEM(tapers.shape, jnp.float32),
            pltpu.VMEM(tapers.shape, jnp.float32),
            pltpu.VMEM((variables, members, owned), jnp.bfloat16),
            pltpu.VMEM((blocks, size, size), jnp.bfloat16),
            pltpu.VMEM((1, owned), jnp.float32),
            pltpu.SMEM((blocks, pairs), jnp.int32),
            pltpu.SMEM((blocks, pairs), jnp.int32),
            pltpu.SemaphoreType.DMA((kinds,)),
            pltpu.SemaphoreType.DMA((kinds,)),
            pltpu.SemaphoreType.DMA((kinds + 2,)),
            pltpu.SemaphoreType.DMA((2, 2)),
            pltpu.SemaphoreType.DMA((2, 2)),
            pltpu.SemaphoreType.DMA,
            pltpu.SemaphoreType.DMA,
            pltpu.SemaphoreType.DMA((4,)),
            pltpu.SemaphoreType.DMA((4,)),
        ],
        compiler_params=pltpu.CompilerParams(collective_id=0, has_side_effects=True),
    )(state, obs_noise, obs_values, obs_weights, tapers, pair_source, pair_taper)


def solution(mesh):
    placed = (
        P(None, "mem", "patch"),
        P("mem", "patch"),
        P("patch", "mem"),
        P("patch", "mem", None, None),
        P(),
        P("patch", "mem", None),
        P("patch", "mem", None),
    )
    return jax.shard_map(
        functools.partial(on_device, mesh.shape["mem"]),
        mesh=mesh,
        in_specs=placed,
        out_specs=P(None, "mem", "patch"),
        check_vma=False,
    )
```

```python
import functools

import jax
import jax.numpy as jnp
from jax import lax
from jax.experimental import pallas as pl
from jax.experimental.pallas import tpu as pltpu
from jax.sharding import PartitionSpec as P

RADIUS = 2
MESH = pl.DeviceIdType.MESH


def gray(q):
    return q + (q // 2) * (1 - 2 * (q % 2))


def device_of(rank, part):
    level, q = rank // 4, rank % 4
    q = q + (level % 2) * (3 - 2 * q)
    spot = gray(q)
    return level * 4 + spot + (part % 2) * (3 - 2 * spot)


def rank_of(device, part):
    level, spot = device // 4, device % 4
    spot = spot + (part % 2) * (3 - 2 * spot)
    q = gray(spot)
    return level * 4 + q + (level % 2) * (3 - 2 * q)


def kernel(
    n,
    state, noise, obs_values, obs_weights, tapers, pair_source, pair_taper,
    out,
    rin, win_at, win_w, anom, local_t, taper_in, taper_t, outbuf, weights_in, values_in, source_in, choice_in,
    in_send, in_recv, local_sem, halo_send, halo_recv, out_send, out_recv, small_send, small_recv,
    guest_in, guest_weights, guest_values, guest_send, guest_recv, guest_local, guest_small_send, guest_small_recv,
):
    me = lax.axis_index("mem")
    part = lax.axis_index("patch")
    variables, rows, _ = state.shape
    members, owned = rin.shape[1], rin.shape[2]
    blocks, size, _ = weights_in.shape
    pairs = source_in.shape[1]
    kinds = rin.shape[0]
    rank = rank_of(me, part)
    low, high = n // 2 - 1, n // 2
    is_guest = jnp.logical_or(rank == low, rank == high)
    across = low + high - rank
    across_start = jnp.where(rank == low, RADIUS + blocks, 0)

    barrier = pltpu.get_barrier_semaphore()

    def greet(k, _):
        peer = lax.rem(me + k, n)
        pl.semaphore_signal(barrier, inc=1, device_id=(peer, part), device_id_type=MESH)
        return 0

    lax.fori_loop(1, n, greet, 0)

    def source(kind, owner):
        columns = pl.ds(pl.multiple_of(owner * owned, owned), owned)
        return noise.at[:, columns] if kind == 1 else state.at[max(kind - 1, 0), :, columns]

    my_rows = pl.ds(pl.multiple_of(me * rows, rows), rows)
    locals_ = [
        pltpu.make_async_copy(source(kind, rank), rin.at[kind, my_rows], local_sem.at[kind])
        for kind in range(kinds)
    ]
    for copy in locals_:
        copy.start()
    taper_copy = pltpu.make_async_copy(tapers, taper_in, local_sem.at[kinds])
    taper_copy.start()
    pl.semaphore_wait(barrier, n - 1)

    def guest_copy(kind):
        return pltpu.make_async_copy(
            source(kind, jnp.clip(across, 0, n - 1)), guest_in.at[kind, my_rows], guest_local.at[kind]
        )

    def send_guests(kind):
        for host, other in ((low, high), (high, low)):
            host_device = device_of(host, part)

            @pl.when(host_device != me)
            def _():
                pltpu.make_async_remote_copy(
                    src_ref=source(kind, other),
                    dst_ref=guest_in.at[kind, my_rows],
                    send_sem=guest_send.at[kind],
                    recv_sem=guest_recv.at[kind],
                    device_id=(host_device, part),
                    device_id_type=MESH,
                ).start()

        @pl.when(is_guest)
        def _():
            guest_copy(kind).start()

    guest_small = [(obs_weights.at[0], guest_weights), (obs_values, guest_values)]
    lends = jnp.logical_or(me == low, me == high)

    def guest_remote(i):
        return pltpu.make_async_remote_copy(
            src_ref=guest_small[i][0],
            dst_ref=guest_small[i][1],
            send_sem=guest_small_send.at[i],
            recv_sem=guest_small_recv.at[i],
            device_id=(device_of(jnp.clip(low + high - me, 0, n - 1), part), part),
            device_id_type=MESH,
        )

    def guest_arrived(kind):
        guest_copy(kind).wait()
        block = guest_in.at[kind, pl.ds(0, (n - 1) * rows)]
        pltpu.make_async_copy(block, block, guest_recv.at[kind]).wait()

    def send_kind(kind):
        def send(k, _):
            peer = lax.rem(me + k, n)
            pltpu.make_async_remote_copy(
                src_ref=source(kind, rank_of(peer, part)),
                dst_ref=rin.at[kind, my_rows],
                send_sem=in_send.at[kind],
                recv_sem=in_recv.at[kind],
                device_id=(peer, part),
                device_id_type=MESH,
            ).start()
            return 0

        lax.fori_loop(1, n, send, 0)

    send_kind(0)
    send_guests(0)
    keeper = device_of(me, part)
    small = [
        (obs_weights.at[0], weights_in),
        (obs_values, values_in),
        (pair_source.at[0], source_in),
        (pair_taper.at[0], choice_in),
    ]

    def small_remote(i):
        return pltpu.make_async_remote_copy(
            src_ref=small[i][0],
            dst_ref=small[i][1],
            send_sem=small_send.at[i],
            recv_sem=small_recv.at[i],
            device_id=(keeper, part),
            device_id_type=MESH,
        )

    def small_local(i):
        return pltpu.make_async_copy(small[i][0], small[i][1], small_recv.at[i])

    @pl.when(keeper != me)
    def _():
        for i in range(len(small)):
            small_remote(i).start()

    @pl.when(keeper == me)
    def _():
        for i in range(len(small)):
            small_local(i).start()

    @pl.when(lends)
    def _():
        for i in range(len(guest_small)):
            guest_remote(i).start()

    send_kind(1)
    send_guests(1)

    taper_copy.wait()
    for k in range(tapers.shape[0]):
        taper_t[k] = taper_in[k].T * (1.0 / (members - 1))

    remote_rows = (n - 1) * rows

    def arrived(kind):
        locals_[kind].wait()
        block = rin.at[kind, pl.ds(0, remote_rows)]
        pltpu.make_async_copy(block, block, in_recv.at[kind]).wait()

    def centered(array):
        values = array.astype(jnp.float32)
        center = jnp.sum(values, axis=0, keepdims=True) * (1.0 / members)
        return (values - center).astype(jnp.bfloat16)

    own = pl.ds(RADIUS, blocks)
    halo = []

    def exchange(window, index):
        left = pltpu.make_async_remote_copy(
            src_ref=window.at[own],
            dst_ref=window.at[pl.ds(RADIUS + blocks, blocks)],
            send_sem=halo_send.at[index, 0],
            recv_sem=halo_recv.at[index, 0],
            device_id=(device_of(jnp.maximum(rank - 1, 0), part), part),
            device_id_type=MESH,
        )
        right = pltpu.make_async_remote_copy(
            src_ref=window.at[own],
            dst_ref=window.at[pl.ds(0, blocks)],
            send_sem=halo_send.at[index, 1],
            recv_sem=halo_recv.at[index, 1],
            device_id=(device_of(jnp.minimum(rank + 1, n - 1), part), part),
            device_id_type=MESH,
        )

        @pl.when(jnp.logical_and(rank > 0, rank != high))
        def _():
            left.start()

        @pl.when(jnp.logical_and(rank < n - 1, rank != low))
        def _():
            right.start()

        halo.append((left, right))

    def landed(index):
        left, right = halo[index]

        @pl.when(jnp.logical_and(rank > 0, rank != high))
        def _():
            left.wait_send()
            right.wait_recv()

        @pl.when(jnp.logical_and(rank < n - 1, rank != low))
        def _():
            right.wait_send()
            left.wait_recv()

    arrived(0)
    first = centered(rin[0])
    anom[0] = first
    for b in range(blocks):
        win_at[RADIUS + b] = first[:, b * size : (b + 1) * size].T
    exchange(win_at, 0)
    send_kind(2)

    @pl.when(keeper != me)
    def _():
        for i in range(len(small)):
            small_remote(i).wait()

    @pl.when(keeper == me)
    def _():
        for i in range(len(small)):
            small_local(i).wait()

    arrived(1)

    def weigh(observed, perturbed, values, weights, start):
        innovation = (
            values[...] + perturbed.astype(jnp.float32) - observed.astype(jnp.float32)
        ).astype(jnp.bfloat16)
        for b in range(blocks):
            win_w[start + b] = lax.dot_general(
                innovation[:, b * size : (b + 1) * size],
                weights[b],
                (((1,), (1,)), ((), ())),
                preferred_element_type=jnp.float32,
            ).astype(jnp.bfloat16)

    weigh(rin[0], rin[1], values_in, weights_in, RADIUS)
    exchange(win_w, 1)
    for kind in range(3, kinds):
        send_kind(kind)

    @pl.when(is_guest)
    def _():
        guest_arrived(0)
        values = centered(guest_in[0])
        for b in range(blocks):
            win_at[across_start + b] = values[:, b * size : (b + 1) * size].T
        for i in range(len(guest_small)):
            guest_remote(i).wait_recv()
        guest_arrived(1)
        weigh(guest_in[0], guest_in[1], guest_values, guest_weights, across_start)

    @pl.when(lends)
    def _():
        for i in range(len(guest_small)):
            guest_remote(i).wait_send()

    base = rank * blocks - RADIUS

    def slot(b, j):
        return jnp.clip(source_in[b, j] - base, 0, win_at.shape[0] - 1)

    chunks = 4
    chunk = members // chunks
    per = chunk // rows
    mine = pl.ds(pl.multiple_of(rank * owned, owned), owned)
    quarter = me // per
    half, odd = quarter // 2, quarter % 2

    def localize(v):
        for b in range(blocks):
            def pair(j, _, b=b):
                covariance = jnp.dot(
                    win_at[slot(b, j)],
                    anom[v, :, b * size : (b + 1) * size],
                    preferred_element_type=jnp.float32,
                )
                local_t[v, b, pl.ds(pl.multiple_of(j * size, size), size), :] = (
                    covariance * taper_t[choice_in[b, j]]
                ).astype(jnp.bfloat16)
                return 0

            lax.fori_loop(0, pairs, pair, 0)

    def answer(v):
        kind = v + 1 if v else 0

        def step(i, _):
            over, flip = i // 2, (i + i // 2) % 2
            at = 2 * (1 - over + (2 * over - 1) * half) + flip + (1 - 2 * flip) * odd
            here = pl.ds(pl.multiple_of(at * chunk, chunk), chunk)
            for b in range(blocks):
                weights = jnp.concatenate(
                    [win_w[slot(b, j), here, :] for j in range(pairs)], axis=1
                )
                increment = jnp.dot(weights, local_t[v, b], preferred_element_type=jnp.float32)
                part_of = slice(b * size, (b + 1) * size)
                outbuf[v, here, part_of] = (
                    rin[kind, here, part_of].astype(jnp.float32) + increment
                ).astype(jnp.bfloat16)

            def give(k, _):
                peer = at * per + lax.rem(k + me, per)
                theirs = pl.ds(pl.multiple_of(peer * rows, rows), rows)

                @pl.when(peer != me)
                def _():
                    pltpu.make_async_remote_copy(
                        src_ref=outbuf.at[v, theirs, :],
                        dst_ref=out.at[v, :, mine],
                        send_sem=out_send,
                        recv_sem=out_recv,
                        device_id=(peer, part),
                        device_id_type=MESH,
                    ).start()

                return 0

            lax.fori_loop(0, per, give, 0)
            return 0

        lax.fori_loop(0, chunks, step, 0)

    for v in range(variables):
        if v:
            arrived(v + 1)
            anom[v] = centered(rin[v + 1])
        else:
            landed(0)
        localize(v)
        if not v:
            landed(1)
        answer(v)

    keep = pltpu.make_async_copy(outbuf.at[:, my_rows, :], out.at[:, :, mine], local_sem.at[kinds + 1])
    keep.start()
    keep.wait()
    for kind in range(2):
        one = guest_in.at[kind, pl.ds(0, rows)]
        both = guest_in.at[kind, pl.ds(0, 2 * rows)]

        @pl.when(is_guest)
        def _():
            pltpu.make_async_copy(one, one, guest_send.at[kind]).wait()

        @pl.when(jnp.logical_not(is_guest))
        def _():
            pltpu.make_async_copy(both, both, guest_send.at[kind]).wait()

    for kind in range(kinds):
        block = rin.at[kind, pl.ds(0, remote_rows)]
        pltpu.make_async_copy(block, block, in_send.at[kind]).wait()
    block = outbuf.at[:, pl.ds(0, remote_rows), :]
    pltpu.make_async_copy(block, block, out_send).wait()
    pltpu.make_async_copy(block, block, out_recv).wait()


def settle(array):
    parts = 6
    depth, rows, cells = array.shape
    width = cells * depth // parts

    def body(given, out, held, came, went):
        def piece(i):
            per = parts // depth
            return i // per, slice(None), pl.ds((i % per) * width, width)

        reads = [pltpu.make_async_copy(given.at[piece(i)], held.at[piece(i)], came.at[i]) for i in range(parts)]
        writes = [pltpu.make_async_copy(held.at[piece(i)], out.at[piece(i)], went.at[i]) for i in range(parts)]
        for copy in reads:
            copy.start()
        for i in range(parts):
            reads[i].wait()
            writes[i].start()
        for copy in writes:
            copy.wait()

    anywhere = pl.BlockSpec(memory_space=pl.ANY)
    return pl.pallas_call(
        body,
        out_shape=jax.ShapeDtypeStruct(array.shape, array.dtype),
        in_specs=[anywhere],
        out_specs=anywhere,
        scratch_shapes=[
            pltpu.VMEM(array.shape, array.dtype),
            pltpu.SemaphoreType.DMA((parts,)),
            pltpu.SemaphoreType.DMA((parts,)),
        ],
    )(array)


def on_device(n, state, obs_noise, obs_values, obs_weights, tapers, pair_source, pair_taper):
    variables, rows, cells = state.shape
    members = rows * n
    owned = cells // n
    blocks, size = obs_weights.shape[1], obs_weights.shape[2]
    pairs = pair_source.shape[2]
    window = blocks + 2 * RADIUS
    anywhere = pl.BlockSpec(memory_space=pl.ANY)
    kinds = variables + 1
    moved = pl.pallas_call(
        functools.partial(kernel, n),
        out_shape=jax.ShapeDtypeStruct(state.shape, state.dtype),
        in_specs=[anywhere] * 7,
        out_specs=anywhere,
        scratch_shapes=[
            pltpu.VMEM((kinds, members, owned), jnp.bfloat16),
            pltpu.VMEM((window, size, members), jnp.bfloat16),
            pltpu.VMEM((window, members, size), jnp.bfloat16),
            pltpu.VMEM((variables, members, owned), jnp.bfloat16),
            pltpu.VMEM((variables, blocks, pairs * size, size), jnp.bfloat16),
            pltpu.VMEM(tapers.shape, jnp.float32),
            pltpu.VMEM(tapers.shape, jnp.float32),
            pltpu.VMEM((variables, members, owned), jnp.bfloat16),
            pltpu.VMEM((blocks, size, size), jnp.bfloat16),
            pltpu.VMEM((1, owned), jnp.float32),
            pltpu.SMEM((blocks, pairs), jnp.int32),
            pltpu.SMEM((blocks, pairs), jnp.int32),
            pltpu.SemaphoreType.DMA((kinds,)),
            pltpu.SemaphoreType.DMA((kinds,)),
            pltpu.SemaphoreType.DMA((kinds + 2,)),
            pltpu.SemaphoreType.DMA((2, 2)),
            pltpu.SemaphoreType.DMA((2, 2)),
            pltpu.SemaphoreType.DMA,
            pltpu.SemaphoreType.DMA,
            pltpu.SemaphoreType.DMA((4,)),
            pltpu.SemaphoreType.DMA((4,)),
            pltpu.VMEM((2, members, owned), jnp.bfloat16),
            pltpu.VMEM((blocks, size, size), jnp.bfloat16),
            pltpu.VMEM((1, owned), jnp.float32),
            pltpu.SemaphoreType.DMA((2,)),
            pltpu.SemaphoreType.DMA((2,)),
            pltpu.SemaphoreType.DMA((2,)),
            pltpu.SemaphoreType.DMA((2,)),
            pltpu.SemaphoreType.DMA((2,)),
        ],
        compiler_params=pltpu.CompilerParams(collective_id=0, has_side_effects=True),
    )(state, obs_noise, obs_values, obs_weights, tapers, pair_source, pair_taper)
    return settle(moved)


def solution(mesh):
    placed = (
        P(None, "mem", "patch"),
        P("mem", "patch"),
        P("patch", "mem"),
        P("patch", "mem", None, None),
        P(),
        P("patch", "mem", None),
        P("patch", "mem", None),
    )
    return jax.shard_map(
        functools.partial(on_device, mesh.shape["mem"]),
        mesh=mesh,
        in_specs=placed,
        out_specs=P(None, "mem", "patch"),
        check_vma=False,
    )
```

```python
import functools

import jax
import jax.numpy as jnp
from jax import lax
from jax.experimental import pallas as pl
from jax.experimental.pallas import tpu as pltpu
from jax.sharding import PartitionSpec as P

RADIUS = 2
MESH = pl.DeviceIdType.MESH


def gray(q):
    return q + (q // 2) * (1 - 2 * (q % 2))


def device_of(rank, part):
    level, q = rank // 4, rank % 4
    q = q + (level % 2) * (3 - 2 * q)
    spot = gray(q)
    return level * 4 + spot + (part % 2) * (3 - 2 * spot)


def rank_of(device, part):
    level, spot = device // 4, device % 4
    spot = spot + (part % 2) * (3 - 2 * spot)
    q = gray(spot)
    return level * 4 + q + (level % 2) * (3 - 2 * q)


def kernel(
    n,
    state, noise, obs_values, obs_weights, tapers, pair_source, pair_taper,
    out,
    rin, win_at, win_w, anom, local_t, taper_in, taper_t, outbuf, weights_in, values_in, source_in, choice_in,
    in_send, in_recv, local_sem, halo_send, halo_recv, out_send, out_recv, small_send, small_recv,
    guest_in, guest_weights, guest_values, guest_send, guest_recv, guest_local, guest_small_send, guest_small_recv,
):
    me = lax.axis_index("mem")
    part = lax.axis_index("patch")
    variables, rows, _ = state.shape
    members, owned = rin.shape[1], rin.shape[2]
    blocks, size, _ = weights_in.shape
    pairs = source_in.shape[1]
    kinds = rin.shape[0]
    rank = rank_of(me, part)
    low, high = n // 2 - 1, n // 2
    is_guest = jnp.logical_or(rank == low, rank == high)
    across = low + high - rank
    across_start = jnp.where(rank == low, RADIUS + blocks, 0)

    barrier = pltpu.get_barrier_semaphore()

    def greet(k, _):
        peer = lax.rem(me + k, n)
        pl.semaphore_signal(barrier, inc=1, device_id=(peer, part), device_id_type=MESH)
        return 0

    lax.fori_loop(1, n, greet, 0)

    def source(kind, owner):
        columns = pl.ds(pl.multiple_of(owner * owned, owned), owned)
        return noise.at[:, columns] if kind == 1 else state.at[max(kind - 1, 0), :, columns]

    my_rows = pl.ds(pl.multiple_of(me * rows, rows), rows)
    locals_ = [
        pltpu.make_async_copy(source(kind, rank), rin.at[kind, my_rows], local_sem.at[kind])
        for kind in range(kinds)
    ]
    for copy in locals_:
        copy.start()
    taper_copy = pltpu.make_async_copy(tapers, taper_in, local_sem.at[kinds])
    taper_copy.start()
    pl.semaphore_wait(barrier, n - 1)

    def guest_copy(kind):
        return pltpu.make_async_copy(
            source(kind, jnp.clip(across, 0, n - 1)), guest_in.at[kind, my_rows], guest_local.at[kind]
        )

    def send_guests(kind):
        for host, other in ((low, high), (high, low)):
            host_device = device_of(host, part)

            @pl.when(host_device != me)
            def _():
                pltpu.make_async_remote_copy(
                    src_ref=source(kind, other),
                    dst_ref=guest_in.at[kind, my_rows],
                    send_sem=guest_send.at[kind],
                    recv_sem=guest_recv.at[kind],
                    device_id=(host_device, part),
                    device_id_type=MESH,
                ).start()

        @pl.when(is_guest)
        def _():
            guest_copy(kind).start()

    guest_small = [(obs_weights.at[0], guest_weights), (obs_values, guest_values)]
    lends = jnp.logical_or(me == low, me == high)

    def guest_remote(i):
        return pltpu.make_async_remote_copy(
            src_ref=guest_small[i][0],
            dst_ref=guest_small[i][1],
            send_sem=guest_small_send.at[i],
            recv_sem=guest_small_recv.at[i],
            device_id=(device_of(jnp.clip(low + high - me, 0, n - 1), part), part),
            device_id_type=MESH,
        )

    def guest_arrived(kind):
        guest_copy(kind).wait()
        block = guest_in.at[kind, pl.ds(0, (n - 1) * rows)]
        pltpu.make_async_copy(block, block, guest_recv.at[kind]).wait()

    def send_kind(kind):
        def send(k, _):
            peer = lax.rem(me + k, n)
            pltpu.make_async_remote_copy(
                src_ref=source(kind, rank_of(peer, part)),
                dst_ref=rin.at[kind, my_rows],
                send_sem=in_send.at[kind],
                recv_sem=in_recv.at[kind],
                device_id=(peer, part),
                device_id_type=MESH,
            ).start()
            return 0

        lax.fori_loop(1, n, send, 0)

    send_kind(0)
    send_guests(0)
    keeper = device_of(me, part)
    small = [
        (obs_weights.at[0], weights_in),
        (obs_values, values_in),
        (pair_source.at[0], source_in),
        (pair_taper.at[0], choice_in),
    ]

    def small_remote(i):
        return pltpu.make_async_remote_copy(
            src_ref=small[i][0],
            dst_ref=small[i][1],
            send_sem=small_send.at[i],
            recv_sem=small_recv.at[i],
            device_id=(keeper, part),
            device_id_type=MESH,
        )

    def small_local(i):
        return pltpu.make_async_copy(small[i][0], small[i][1], small_recv.at[i])

    @pl.when(keeper != me)
    def _():
        for i in range(len(small)):
            small_remote(i).start()

    @pl.when(keeper == me)
    def _():
        for i in range(len(small)):
            small_local(i).start()

    @pl.when(lends)
    def _():
        for i in range(len(guest_small)):
            guest_remote(i).start()

    send_kind(1)
    send_guests(1)

    taper_copy.wait()
    for k in range(tapers.shape[0]):
        taper_t[k] = taper_in[k].T * (1.0 / (members - 1))

    remote_rows = (n - 1) * rows

    def arrived(kind):
        locals_[kind].wait()
        block = rin.at[kind, pl.ds(0, remote_rows)]
        pltpu.make_async_copy(block, block, in_recv.at[kind]).wait()

    def centered(array):
        values = array.astype(jnp.float32)
        center = jnp.sum(values, axis=0, keepdims=True) * (1.0 / members)
        return (values - center).astype(jnp.bfloat16)

    own = pl.ds(RADIUS, blocks)
    halo = []

    def exchange(window, index):
        left = pltpu.make_async_remote_copy(
            src_ref=window.at[own],
            dst_ref=window.at[pl.ds(RADIUS + blocks, blocks)],
            send_sem=halo_send.at[index, 0],
            recv_sem=halo_recv.at[index, 0],
            device_id=(device_of(jnp.maximum(rank - 1, 0), part), part),
            device_id_type=MESH,
        )
        right = pltpu.make_async_remote_copy(
            src_ref=window.at[own],
            dst_ref=window.at[pl.ds(0, blocks)],
            send_sem=halo_send.at[index, 1],
            recv_sem=halo_recv.at[index, 1],
            device_id=(device_of(jnp.minimum(rank + 1, n - 1), part), part),
            device_id_type=MESH,
        )

        @pl.when(jnp.logical_and(rank > 0, rank != high))
        def _():
            left.start()

        @pl.when(jnp.logical_and(rank < n - 1, rank != low))
        def _():
            right.start()

        halo.append((left, right))

    def landed(index):
        left, right = halo[index]

        @pl.when(jnp.logical_and(rank > 0, rank != high))
        def _():
            left.wait_send()
            right.wait_recv()

        @pl.when(jnp.logical_and(rank < n - 1, rank != low))
        def _():
            right.wait_send()
            left.wait_recv()

    arrived(0)
    first = centered(rin[0])
    anom[0] = first
    for b in range(blocks):
        win_at[RADIUS + b] = first[:, b * size : (b + 1) * size].T
    exchange(win_at, 0)
    send_kind(2)

    @pl.when(keeper != me)
    def _():
        for i in range(len(small)):
            small_remote(i).wait()

    @pl.when(keeper == me)
    def _():
        for i in range(len(small)):
            small_local(i).wait()

    arrived(1)

    def weigh(observed, perturbed, values, weights, start):
        innovation = (
            values[...] + perturbed.astype(jnp.float32) - observed.astype(jnp.float32)
        ).astype(jnp.bfloat16)
        for b in range(blocks):
            win_w[start + b] = lax.dot_general(
                innovation[:, b * size : (b + 1) * size],
                weights[b],
                (((1,), (1,)), ((), ())),
                preferred_element_type=jnp.float32,
            ).astype(jnp.bfloat16)

    weigh(rin[0], rin[1], values_in, weights_in, RADIUS)
    exchange(win_w, 1)

    @pl.when(is_guest)
    def _():
        guest_arrived(0)
        values = centered(guest_in[0])
        for b in range(blocks):
            win_at[across_start + b] = values[:, b * size : (b + 1) * size].T
        for i in range(len(guest_small)):
            guest_remote(i).wait_recv()
        guest_arrived(1)
        weigh(guest_in[0], guest_in[1], guest_values, guest_weights, across_start)

    @pl.when(lends)
    def _():
        for i in range(len(guest_small)):
            guest_remote(i).wait_send()

    base = rank * blocks - RADIUS

    def slot(b, j):
        return jnp.clip(source_in[b, j] - base, 0, win_at.shape[0] - 1)

    chunks = 4
    chunk = members // chunks
    per = chunk // rows
    mine = pl.ds(pl.multiple_of(rank * owned, owned), owned)
    quarter = me // per
    half, odd = quarter // 2, quarter % 2

    def localize(v):
        for b in range(blocks):
            def pair(j, _, b=b):
                covariance = jnp.dot(
                    win_at[slot(b, j)],
                    anom[v, :, b * size : (b + 1) * size],
                    preferred_element_type=jnp.float32,
                )
                local_t[v, b, pl.ds(pl.multiple_of(j * size, size), size), :] = (
                    covariance * taper_t[choice_in[b, j]]
                ).astype(jnp.bfloat16)
                return 0

            lax.fori_loop(0, pairs, pair, 0)

    def answer(v):
        kind = v + 1 if v else 0

        def step(i, _):
            over, flip = i // 2, (i + i // 2) % 2
            at = 2 * (1 - over + (2 * over - 1) * half) + flip + (1 - 2 * flip) * odd
            here = pl.ds(pl.multiple_of(at * chunk, chunk), chunk)
            for b in range(blocks):
                weights = jnp.concatenate(
                    [win_w[slot(b, j), here, :] for j in range(pairs)], axis=1
                )
                increment = jnp.dot(weights, local_t[v, b], preferred_element_type=jnp.float32)
                part_of = slice(b * size, (b + 1) * size)
                outbuf[v, here, part_of] = (
                    rin[kind, here, part_of].astype(jnp.float32) + increment
                ).astype(jnp.bfloat16)

            def give(k, _):
                peer = at * per + lax.rem(k + me, per)
                theirs = pl.ds(pl.multiple_of(peer * rows, rows), rows)

                @pl.when(peer != me)
                def _():
                    pltpu.make_async_remote_copy(
                        src_ref=outbuf.at[v, theirs, :],
                        dst_ref=out.at[v, :, mine],
                        send_sem=out_send,
                        recv_sem=out_recv,
                        device_id=(peer, part),
                        device_id_type=MESH,
                    ).start()

                return 0

            lax.fori_loop(0, per, give, 0)
            return 0

        lax.fori_loop(0, chunks, step, 0)

    for v in range(variables):
        if v:
            arrived(v + 1)
            anom[v] = centered(rin[v + 1])
        else:
            landed(0)
        localize(v)
        if not v:
            for kind in range(3, kinds):
                send_kind(kind)
            landed(1)
        answer(v)

    keep = pltpu.make_async_copy(outbuf.at[:, my_rows, :], out.at[:, :, mine], local_sem.at[kinds + 1])
    keep.start()
    keep.wait()
    for kind in range(2):
        one = guest_in.at[kind, pl.ds(0, rows)]
        both = guest_in.at[kind, pl.ds(0, 2 * rows)]

        @pl.when(is_guest)
        def _():
            pltpu.make_async_copy(one, one, guest_send.at[kind]).wait()

        @pl.when(jnp.logical_not(is_guest))
        def _():
            pltpu.make_async_copy(both, both, guest_send.at[kind]).wait()

    for kind in range(kinds):
        block = rin.at[kind, pl.ds(0, remote_rows)]
        pltpu.make_async_copy(block, block, in_send.at[kind]).wait()
    block = outbuf.at[:, pl.ds(0, remote_rows), :]
    pltpu.make_async_copy(block, block, out_send).wait()
    pltpu.make_async_copy(block, block, out_recv).wait()


def settle(array):
    parts = 6
    depth, rows, cells = array.shape
    width = cells * depth // parts

    def body(given, out, held, came, went):
        def piece(i):
            per = parts // depth
            return i // per, slice(None), pl.ds((i % per) * width, width)

        reads = [pltpu.make_async_copy(given.at[piece(i)], held.at[piece(i)], came.at[i]) for i in range(parts)]
        writes = [pltpu.make_async_copy(held.at[piece(i)], out.at[piece(i)], went.at[i]) for i in range(parts)]
        for copy in reads:
            copy.start()
        for i in range(parts):
            reads[i].wait()
            writes[i].start()
        for copy in writes:
            copy.wait()

    anywhere = pl.BlockSpec(memory_space=pl.ANY)
    return pl.pallas_call(
        body,
        out_shape=jax.ShapeDtypeStruct(array.shape, array.dtype),
        in_specs=[anywhere],
        out_specs=anywhere,
        scratch_shapes=[
            pltpu.VMEM(array.shape, array.dtype),
            pltpu.SemaphoreType.DMA((parts,)),
            pltpu.SemaphoreType.DMA((parts,)),
        ],
    )(array)


def on_device(n, state, obs_noise, obs_values, obs_weights, tapers, pair_source, pair_taper):
    variables, rows, cells = state.shape
    members = rows * n
    owned = cells // n
    blocks, size = obs_weights.shape[1], obs_weights.shape[2]
    pairs = pair_source.shape[2]
    window = blocks + 2 * RADIUS
    anywhere = pl.BlockSpec(memory_space=pl.ANY)
    kinds = variables + 1
    moved = pl.pallas_call(
        functools.partial(kernel, n),
        out_shape=jax.ShapeDtypeStruct(state.shape, state.dtype),
        in_specs=[anywhere] * 7,
        out_specs=anywhere,
        scratch_shapes=[
            pltpu.VMEM((kinds, members, owned), jnp.bfloat16),
            pltpu.VMEM((window, size, members), jnp.bfloat16),
            pltpu.VMEM((window, members, size), jnp.bfloat16),
            pltpu.VMEM((variables, members, owned), jnp.bfloat16),
            pltpu.VMEM((variables, blocks, pairs * size, size), jnp.bfloat16),
            pltpu.VMEM(tapers.shape, jnp.float32),
            pltpu.VMEM(tapers.shape, jnp.float32),
            pltpu.VMEM((variables, members, owned), jnp.bfloat16),
            pltpu.VMEM((blocks, size, size), jnp.bfloat16),
            pltpu.VMEM((1, owned), jnp.float32),
            pltpu.SMEM((blocks, pairs), jnp.int32),
            pltpu.SMEM((blocks, pairs), jnp.int32),
            pltpu.SemaphoreType.DMA((kinds,)),
            pltpu.SemaphoreType.DMA((kinds,)),
            pltpu.SemaphoreType.DMA((kinds + 2,)),
            pltpu.SemaphoreType.DMA((2, 2)),
            pltpu.SemaphoreType.DMA((2, 2)),
            pltpu.SemaphoreType.DMA,
            pltpu.SemaphoreType.DMA,
            pltpu.SemaphoreType.DMA((4,)),
            pltpu.SemaphoreType.DMA((4,)),
            pltpu.VMEM((2, members, owned), jnp.bfloat16),
            pltpu.VMEM((blocks, size, size), jnp.bfloat16),
            pltpu.VMEM((1, owned), jnp.float32),
            pltpu.SemaphoreType.DMA((2,)),
            pltpu.SemaphoreType.DMA((2,)),
            pltpu.SemaphoreType.DMA((2,)),
            pltpu.SemaphoreType.DMA((2,)),
            pltpu.SemaphoreType.DMA((2,)),
        ],
        compiler_params=pltpu.CompilerParams(collective_id=0, has_side_effects=True),
    )(state, obs_noise, obs_values, obs_weights, tapers, pair_source, pair_taper)
    return settle(moved)


def solution(mesh):
    placed = (
        P(None, "mem", "patch"),
        P("mem", "patch"),
        P("patch", "mem"),
        P("patch", "mem", None, None),
        P(),
        P("patch", "mem", None),
        P("patch", "mem", None),
    )
    return jax.shard_map(
        functools.partial(on_device, mesh.shape["mem"]),
        mesh=mesh,
        in_specs=placed,
        out_specs=P(None, "mem", "patch"),
        check_vma=False,
    )
```
